32 devices in a mesh: dp: 8 (over z, x), bn: 4 (over y, core).
Axes of the slice: x: 2, y: 2, z: 4, core: 2. Of those that a mesh axis runs over, the one named last changes fastest.
Arguments:
- features: bfloat16 [512, 8, 2048], P(('dp', 'bn')), may hold values from -6 to 6
- shuffle_masks: int32 [16], replicated, may hold values from 0 to 7, as said below
- conv_in: bfloat16 [2048, 512], replicated, may hold values from -0.125 to 0.125
- conv_mid: bfloat16 [3, 512, 512], replicated, may hold values from -0.15625 to 0.15625
- conv_out: bfloat16 [512, 2048], replicated, may hold values from -0.25 to 0.25
- head: bfloat16 [2048, 128], replicated, may hold values from -0.125 to 0.125
- queries: bfloat16 [512, 128], P(('dp', 'bn'))
- queue: bfloat16 [65536, 128], P('dp')
- positive: int32 [512], P(('dp', 'bn')), may hold values from 0 to 511, as said below
Outputs:
- loss_rows: float32 [512], P(('dp', 'bn'))
The draws below stay inside these ranges and needn't reach their ends.
Inputs may be any that keep to these rules, and one draw needn't show every extreme that they name: `shuffle_masks`: every binary digit of a dp index is set in exactly half of the entries. positive[i] names a crop with the same bn index as crop i.
All inputs are finite; a program needn't handle non-finite values.
Results may differ from the reference program's by a relative error of at most 0.0023.
Values may be sent and summed in bfloat16 or wider, within the bound.
A program may use at most 64 MiB of HBM per device.

```python
import math
import jax
import jax.numpy as jnp
from jax import lax

CH = 2048
MID = 512
EMB = 128
QUEUE = 65536
POS = 8
CROP_DEV = 16
CROPS = 512
DP_BITS = 3
N_DP = 8
N_BN = 4


def query_base(key):
    base_rows = jax.random.normal(jax.random.fold_in(key, 11), (CROPS, EMB), jnp.float32)
    return base_rows


def draw_queries(key, part):
    base_rows = query_base(key)
    return base_rows.astype(jnp.bfloat16)


def draw_queue(key, part):
    base_rows = query_base(key)
    owner_row = jax.random.randint(jax.random.fold_in(key, 13), (QUEUE,), 0, CROPS, jnp.int32)
    planted_mask = jax.random.randint(jax.random.fold_in(key, 16), (QUEUE,), 0, 2, jnp.int32) == 1
    noise_rows = jax.random.normal(jax.random.fold_in(key, 14), (QUEUE, EMB), jnp.float32)
    noise_level = jax.random.uniform(jax.random.fold_in(key, 17), (QUEUE, 1), jnp.float32, 0.08, 0.4)
    planted = jnp.take(base_rows, owner_row, axis=0) + noise_level * noise_rows
    queue_rows = jnp.where(planted_mask[:, None], planted, noise_rows)
    return queue_rows.astype(jnp.bfloat16)


def draw_shuffle_masks(key, part):
    half = CROP_DEV // 2
    total = jnp.zeros((CROP_DEV,), jnp.int32)
    for level in range(DP_BITS):
        order = jax.random.permutation(jax.random.fold_in(key, 40 + level), CROP_DEV - 2).astype(jnp.int32) + 2
        chosen = jnp.concatenate([jnp.zeros((1,), jnp.int32), order[:half - 1]])
        flags = jnp.zeros((CROP_DEV,), jnp.int32).at[chosen].set(1)
        total = total + flags * 2 ** level
    return total


def draw_positive(key, part):
    crop_ids = jnp.arange(CROPS, dtype=jnp.int32)
    group_of = crop_ids // CROP_DEV % N_BN
    column = jax.random.randint(jax.random.fold_in(key, 31), (CROPS,), 0, N_DP, jnp.int32)
    slot_of = jax.random.randint(jax.random.fold_in(key, 32), (CROPS,), 0, CROP_DEV, jnp.int32)
    picked = (column * N_BN + group_of) * CROP_DEV + slot_of
    picked = picked.at[0].set(0)
    return picked.at[CROPS - 1].set(CROPS - 1)


def block_scale(key, shape, shards, low, top_value):
    loudness = 1.0
    for position, shards_of in shards:
        heights = jax.random.uniform(jax.random.fold_in(jax.random.fold_in(key, 6), position), (shards_of,), jnp.float32, low / len(shards), top_value / len(shards))
        loudness = loudness * jnp.repeat(jnp.exp(heights), shape[position] // shards_of).reshape((-1,) + (1,) * (len(shape) - 1 - position))
    return loudness


def bell_draw(rng, dims, scale, limit, cuts=(), kind=jnp.bfloat16):
    drawn = scale * jax.random.normal(rng, dims, jnp.float32)
    if cuts:
        drawn = drawn * block_scale(rng, dims, cuts, -0.22, 0.18)
    return jnp.clip(drawn, -limit, limit).astype(kind)


def setup_inputs(seed: int = 0) -> dict:
    arg_keys = jax.random.split(jax.random.key(seed), 10)
    features = bell_draw(arg_keys[0], (CROPS, POS, CH), 1.0, 6.0, ((0, 32),))
    shuffle_masks = draw_shuffle_masks(jax.random.fold_in(arg_keys[9], 71), 0)
    conv_in = bell_draw(arg_keys[2], (CH, MID), CH ** -0.5, 0.125)
    conv_mid = bell_draw(arg_keys[3], (3, MID, MID), (3 * MID) ** -0.5, 0.15625)
    conv_out = bell_draw(arg_keys[4], (MID, CH), MID ** -0.5, 0.25)
    head = bell_draw(arg_keys[5], (CH, EMB), CH ** -0.5, 0.125)
    queries = draw_queries(jax.random.fold_in(arg_keys[9], 71), 0)
    queue = draw_queue(jax.random.fold_in(arg_keys[9], 71), 0)
    positive = draw_positive(jax.random.fold_in(arg_keys[9], 71), 0)
    return {"features": features, "shuffle_masks": shuffle_masks, "conv_in": conv_in, "conv_mid": conv_mid, "conv_out": conv_out, "head": head, "queries": queries, "queue": queue, "positive": positive}


EPS_BN = 1e-05
EPS_UNIT = 1e-06
INV_TEMP = 1.0 / 0.07

def unit_rows(values):
    values = values.astype(jnp.float32)
    return values * lax.rsqrt(lax.optimization_barrier(jnp.sum(values * values, axis=-1, keepdims=True)) + EPS_UNIT)

def group_norm(values):
    center = lax.optimization_barrier(jnp.mean(values, axis=1, keepdims=True))
    spread = lax.optimization_barrier(jnp.mean(jnp.square(values - center), axis=1, keepdims=True))
    return (values - center) * lax.rsqrt(spread + EPS_BN)

def project(values, weight):
    shaped = values.reshape(-1, values.shape[-1])
    out = jnp.dot(shaped, weight, preferred_element_type=jnp.float32)
    return out.reshape(values.shape[:-1] + (weight.shape[1],))

def reference(features, shuffle_masks, conv_in, conv_mid, conv_out, head, queries, queue, positive):
    dp_ids = jnp.arange(N_DP, dtype=jnp.int32)
    source = jnp.bitwise_xor(dp_ids[:, None], shuffle_masks[None, :].astype(jnp.int32))
    bn_ids = jnp.arange(N_BN, dtype=jnp.int32)[None, :, None]
    slot_ids = jnp.arange(CROP_DEV, dtype=jnp.int32)[None, None, :]
    feature_grid = features.reshape(N_DP, N_BN, CROP_DEV, POS, CH)
    shuffled = feature_grid[source[:, None, :], bn_ids, slot_ids]
    flat_rows = shuffled.reshape(N_DP, N_BN * CROP_DEV * POS, CH)
    first_act = jax.nn.relu(group_norm(project(flat_rows, conv_in))).astype(jnp.bfloat16)
    tap_maps = first_act.reshape(N_DP, N_BN * CROP_DEV, POS, MID)
    padded = jnp.pad(tap_maps, ((0, 0), (0, 0), (1, 1), (0, 0)))
    second_sum = jnp.zeros((N_DP, N_BN * CROP_DEV, POS, MID), jnp.float32)
    for tap in range(3):
        second_sum = second_sum + project(padded[:, :, tap:tap + POS, :], conv_mid[tap])
    second_act = jax.nn.relu(group_norm(second_sum.reshape(N_DP, -1, MID))).astype(jnp.bfloat16)
    third_sum = project(second_act, conv_out)
    block = jax.nn.relu(group_norm(third_sum) + flat_rows.astype(jnp.float32)).astype(jnp.bfloat16)
    pooled = lax.optimization_barrier(jnp.mean(block.reshape(N_DP, N_BN * CROP_DEV, POS, CH).astype(jnp.float32), axis=2)).astype(jnp.bfloat16)
    key_unit = unit_rows(project(pooled, head)).astype(jnp.bfloat16)
    key_grid = key_unit.reshape(N_DP, N_BN, CROP_DEV, EMB)
    restored = key_grid[source[:, None, :], bn_ids, slot_ids].reshape(CROPS, EMB)
    query_unit = unit_rows(queries).astype(jnp.bfloat16)
    queue_unit = unit_rows(queue).astype(jnp.bfloat16)
    picked = jnp.take(restored, positive.astype(jnp.int32), axis=0)
    positive_logit = lax.optimization_barrier(jnp.sum(query_unit.astype(jnp.float32) * picked.astype(jnp.float32), axis=-1)) * INV_TEMP
    block_rows = math.gcd(CROPS, 256)
    blocks = query_unit.reshape(CROPS // block_rows, block_rows, EMB)

    def queue_terms(query_block):
        scores = jnp.dot(query_block, queue_unit.T, preferred_element_type=jnp.float32) * INV_TEMP
        return lax.optimization_barrier(jnp.sum(jnp.exp(scores - INV_TEMP), axis=1))
    negative = lax.map(queue_terms, blocks).reshape(CROPS)
    return jnp.log(jnp.exp(positive_logit - INV_TEMP) + negative) + INV_TEMP - positive_logit
```

```python
import functools

import jax
import jax.numpy as jnp
from jax import lax
from jax.experimental import pallas as pl
from jax.experimental.pallas import tpu as pltpu
from jax.sharding import PartitionSpec as P

EPS_BN = 1e-05
EPS_UNIT = 1e-06
INV_TEMP = 1.0 / 0.07


def partner_2(value, axis, distance):
    return lax.ppermute(value, axis, [(i, i ^ 1 << distance) for i in range(lax.axis_size(axis))])


def unit_rows(values):
    values = values.astype(jnp.float32)
    return values * lax.rsqrt(jnp.sum(values * values, axis=-1, keepdims=True) + EPS_UNIT)


def group_norm(values, row_total):
    first = lax.psum(jnp.sum(values, axis=0), "bn")
    center = first / row_total
    spread = lax.psum(jnp.sum(jnp.square(values - center), axis=0), "bn") / row_total
    return (values - center) * lax.rsqrt(spread + EPS_BN)


def moving_slots(shuffle_masks, level, half):
    flags = jnp.bitwise_and(jnp.right_shift(shuffle_masks, level), 1)
    return jnp.argsort(1 - flags, stable=True)[:half]


def on_device_moving(features, shuffle_masks, conv_in, conv_mid, conv_out, head, queries, queue, positive):
    dp_count = lax.axis_size("dp")
    bn_count = lax.axis_size("bn")
    bit_count = dp_count.bit_length() - 1
    crop_dev, positions, channels = features.shape
    half = crop_dev // 2
    middle = conv_in.shape[1]
    query_unit = unit_rows(queries).astype(jnp.bfloat16)
    query_all = lax.all_gather(query_unit, "dp", axis=0, tiled=True)
    shuffled = features
    for level in range(bit_count):
        moving = moving_slots(shuffle_masks, level, half)
        partner = partner_2(jnp.take(shuffled, moving, axis=0), "dp", level)
        shuffled = shuffled.at[moving].set(partner)
    row_total = crop_dev * positions * bn_count
    flat_rows = shuffled.reshape(crop_dev * positions, channels)
    first_sum = jnp.dot(flat_rows, conv_in, preferred_element_type=jnp.float32)
    first_act = jax.nn.relu(group_norm(first_sum, row_total)).astype(jnp.bfloat16)
    tap_maps = first_act.reshape(crop_dev, positions, middle)
    padded = jnp.pad(tap_maps, ((0, 0), (1, 1), (0, 0)))
    stacked = jnp.concatenate([padded[:, tap : tap + positions, :] for tap in range(3)], axis=2)
    second_sum = jnp.dot(
        stacked.reshape(crop_dev * positions, 3 * middle),
        conv_mid.reshape(3 * middle, middle),
        preferred_element_type=jnp.float32,
    )
    second_act = jax.nn.relu(group_norm(second_sum, row_total)).astype(jnp.bfloat16)
    third_sum = jnp.dot(second_act, conv_out, preferred_element_type=jnp.float32)
    block = jax.nn.relu(group_norm(third_sum, row_total) + flat_rows.astype(jnp.float32)).astype(
        jnp.bfloat16
    )
    pooled = jnp.mean(
        block.reshape(crop_dev, positions, channels).astype(jnp.float32), axis=1
    ).astype(jnp.bfloat16)
    key_unit = unit_rows(jnp.dot(pooled, head, preferred_element_type=jnp.float32)).astype(
        jnp.bfloat16
    )
    for level in range(bit_count):
        moving = moving_slots(shuffle_masks, level, half)
        partner = partner_2(jnp.take(key_unit, moving, axis=0), "dp", level)
        key_unit = key_unit.at[moving].set(partner)
    queue_unit = unit_rows(queue).astype(jnp.bfloat16)
    scores = jnp.dot(query_all, queue_unit.T, preferred_element_type=jnp.float32) * INV_TEMP
    queue_part = jnp.sum(jnp.exp(scores - INV_TEMP), axis=1)
    key_all = lax.all_gather(key_unit, "dp", axis=0, tiled=True)
    slot_of = positive % crop_dev
    column = positive // crop_dev // bn_count
    picked = jnp.take(key_all, column * crop_dev + slot_of, axis=0)
    positive_logit = (
        jnp.sum(query_unit.astype(jnp.float32) * picked.astype(jnp.float32), axis=-1) * INV_TEMP
    )
    negative = lax.psum_scatter(queue_part, "dp", scatter_dimension=0, tiled=True)
    return jnp.log(jnp.exp(positive_logit - INV_TEMP) + negative) + INV_TEMP - positive_logit


MESH = pl.DeviceIdType.MESH
LANES = 128
QUEUE_STEPS = 8
PHASES = ("query", "sum1", "norm1", "sum2", "norm2", "sum3", "norm3", "queue", "key")


def fixed_kernel(
    n_dp, n_bn,
    masks, positive, queries, x_hbm, in_hbm, mid_hbm, out_hbm, head_hbm, queue_hbm,
    loss_ref,
    x_ref, in_ref, mid_ref, out_ref, head_ref, queue_ref,
    h_ref, wide_ref, mean_ref, scale_ref,
    send1, recv1, own1, stat1, send2, recv2, own2, stat2, send3, recv3, own3, stat3,
    query_own, query_all, part_own, part_all, key_own, key_all,
    load_sem, send_sem, recv_sem,
):
    f32, bf16 = jnp.float32, jnp.bfloat16
    n_dev = n_dp * n_bn
    d = lax.axis_index("dp")
    b = lax.axis_index("bn")
    me = d * n_bn + b
    rows, channels = x_ref.shape
    slots = masks.shape[0]
    cells = rows // slots
    middle = in_ref.shape[1]
    total = float(rows * n_bn)

    loads = [
        pltpu.make_async_copy(src, dst, load_sem.at[i])
        for i, (src, dst) in enumerate(
            [(x_hbm, x_ref), (in_hbm, in_ref), (queue_hbm, queue_ref), (mid_hbm, mid_ref), (out_hbm, out_ref), (head_hbm, head_ref)]
        )
    ]
    for load in loads:
        load.start()

    barrier = pltpu.get_barrier_semaphore()

    def greet(k, carry):
        t = (me + k) % n_dev
        pl.semaphore_signal(barrier, inc=1, device_id=(t // n_bn, t % n_bn), device_id_type=MESH)
        return carry

    lax.fori_loop(1, n_dev, greet, 0)

    lane = lax.broadcasted_iota(jnp.int32, (slots, slots), 1)
    sub = lax.broadcasted_iota(jnp.int32, (slots, slots), 0)
    mask_row = jnp.zeros((slots, slots), jnp.int32)
    mask_col = jnp.zeros((slots, slots), jnp.int32)
    pos_row = jnp.zeros((1, slots), jnp.int32)
    lane1 = lax.broadcasted_iota(jnp.int32, (1, slots), 1)
    groups = []
    for s in range(slots):
        groups.append(masks[s] ^ d)
        mask_row = jnp.where(lane == s, groups[s], mask_row)
        mask_col = jnp.where(sub == s, groups[s], mask_col)
        pos_row = jnp.where(lane1 == s, positive[s], pos_row)
    same = (mask_row == mask_col).astype(f32)
    local_mean = same / (jnp.sum(same, axis=0, keepdims=True) * float(cells))
    member = (mask_row[:n_dp] == sub[:n_dp]).astype(f32) if n_dp <= slots else None
    counts = []
    for e in range(n_dp):
        want = e ^ d
        count = jnp.int32(0)
        for s in range(slots):
            count = count + (masks[s] == want).astype(jnp.int32)
        counts.append((count * cells).astype(f32))

    q = queries[...].astype(f32)
    query_unit = (q * lax.rsqrt(jnp.sum(q * q, axis=-1, keepdims=True) + EPS_UNIT)).astype(bf16)
    query_own[...] = query_unit
    query_all[d] = query_unit

    pl.semaphore_wait(barrier, n_dev - 1)

    def all_peers(phase, src_of, dst):
        i = PHASES.index(phase)

        def step(k, carry):
            t = (me + k) % n_dev
            pltpu.make_async_remote_copy(
                src_ref=src_of(t // n_bn, t % n_bn), dst_ref=dst.at[me],
                send_sem=send_sem.at[i], recv_sem=recv_sem.at[i],
                device_id=(t // n_bn, t % n_bn), device_id_type=MESH,
            ).start()
            return carry

        lax.fori_loop(1, n_dev, step, 0)

    def column_peers(phase, src, dst):
        i = PHASES.index(phase)

        def step(k, carry):
            t = (d + k) % n_dp
            pltpu.make_async_remote_copy(
                src_ref=src, dst_ref=dst.at[d],
                send_sem=send_sem.at[i], recv_sem=recv_sem.at[i],
                device_id=(t, b), device_id_type=MESH,
            ).start()
            return carry

        lax.fori_loop(1, n_dp, step, 0)

    def arrived(phase, dst):
        most = dst.at[pl.ds(0, dst.shape[0] - 1)]
        pltpu.make_async_copy(most, most, recv_sem.at[PHASES.index(phase)]).wait()

    def sent(phase, dst):
        most = dst.at[pl.ds(0, dst.shape[0] - 1)]
        pltpu.make_async_copy(most, most, send_sem.at[PHASES.index(phase)]).wait()

    def exact(a, c):
        return jnp.dot(a, c, preferred_element_type=f32, precision=lax.Precision.HIGHEST)

    def send_sums(phase, h, send, recv):
        width = h.shape[1]
        block = width // n_bn
        subs = block // LANES
        shaped = h.reshape(slots, cells, width)
        sums = jnp.sum(shaped, axis=1)
        center = exact(local_mean, sums)
        squares = jnp.sum(jnp.square(shaped - center[:, None, :]), axis=1)
        for at, values in ((0, exact(member, sums)), (subs, exact(member, squares))):
            for j in range(n_bn):
                for r in range(subs):
                    low = j * block + r * LANES
                    send[:, j, at + r, :] = values[:, low : low + LANES]
        recv[me] = send[d, b]
        all_peers(phase, lambda g, j: send.at[g, j], recv)

    def send_norm(phase_in, phase_out, recv, own, stat):
        arrived(phase_in, recv)
        subs = recv.shape[1] // 2
        both = jnp.sum(recv[...], axis=0)
        mean = both[:subs] * (1.0 / total)
        spread = both[subs:]
        for e in range(n_dp):
            part = recv[e * n_bn : (e + 1) * n_bn][:, :subs]
            off = jnp.sum(jnp.square(part - counts[e] * mean[None]), axis=0)
            spread = spread + off / jnp.maximum(counts[e], 1.0)
        own[:subs] = mean
        own[subs:] = lax.rsqrt(spread * (1.0 / total) + EPS_BN)
        stat[me] = own[...]
        all_peers(phase_out, lambda g, j: own, stat)

    def tables(phase, stat, width):
        arrived(phase, stat)
        block = width // n_bn
        subs = block // LANES
        held = stat[...].reshape(n_dp, n_bn, 2 * subs, LANES)
        for j in range(n_bn):
            for r in range(subs):
                low = j * block + r * LANES
                mean_ref[:, low : low + LANES] = held[:, j, r, :]
                scale_ref[:, low : low + LANES] = held[:, j, subs + r, :]

    def slot_row(table, s, width):
        return jnp.broadcast_to(table[pl.ds(groups[s], 1), :width], (cells, width))

    ones = jnp.ones((LANES, LANES), bf16)
    step_rows = queue_ref.shape[0] // QUEUE_STEPS

    def queue_step(c, total_part):
        raw = queue_ref[pl.ds(c * step_rows, step_rows), :].astype(f32)
        square = raw * raw
        high = square.astype(bf16)
        low = (square - high.astype(f32)).astype(bf16)
        norm = jnp.dot(high, ones, preferred_element_type=f32) + jnp.dot(low, ones, preferred_element_type=f32)
        unit = (raw * lax.rsqrt(norm + EPS_UNIT)).astype(bf16)
        flat_queries = query_all[...].reshape(n_dp * slots, query_all.shape[2])
        scores = lax.dot_general(unit, flat_queries, (((1,), (1,)), ((), ())), preferred_element_type=f32)
        terms = jnp.exp(scores * INV_TEMP - INV_TEMP)
        return total_part + jnp.sum(terms.reshape(step_rows // 8, 8, n_dp * slots), axis=0)

    def queue_steps(first, last, total_part):
        return lax.fori_loop(first, last, queue_step, total_part)

    column_peers("query", query_own, query_all)

    loads[0].wait()
    loads[1].wait()
    h_ref[...] = jnp.dot(x_ref[...], in_ref[...], preferred_element_type=f32)
    send_sums("sum1", h_ref[...], send1, recv1)
    part = jnp.zeros((8, n_dp * slots), f32)
    loads[2].wait()
    arrived("query", query_all)
    part = queue_steps(0, 2, part)
    send_norm("sum1", "norm1", recv1, own1, stat1)
    loads[3].wait()
    part = queue_steps(2, 3, part)
    tables("norm1", stat1, middle)

    for s in range(slots):
        at = slice(s * cells, (s + 1) * cells)
        h_ref[at] = jax.nn.relu((h_ref[at] - slot_row(mean_ref, s, middle)) * slot_row(scale_ref, s, middle))
    act = h_ref[...]
    cell = lax.broadcasted_iota(jnp.int32, act.shape, 0) % cells
    before = jnp.where(cell == 0, 0.0, pltpu.roll(act, 1, 0)).astype(bf16)
    after = jnp.where(cell == cells - 1, 0.0, pltpu.roll(act, rows - 1, 0)).astype(bf16)
    h_ref[...] = (
        jnp.dot(before, mid_ref[0], preferred_element_type=f32)
        + jnp.dot(act.astype(bf16), mid_ref[1], preferred_element_type=f32)
        + jnp.dot(after, mid_ref[2], preferred_element_type=f32)
    )
    send_sums("sum2", h_ref[...], send2, recv2)
    part = queue_steps(3, 5, part)
    send_norm("sum2", "norm2", recv2, own2, stat2)
    loads[4].wait()
    part = queue_steps(5, 6, part)
    tables("norm2", stat2, middle)

    for s in range(slots):
        at = slice(s * cells, (s + 1) * cells)
        h_ref[at] = jax.nn.relu((h_ref[at] - slot_row(mean_ref, s, middle)) * slot_row(scale_ref, s, middle))
    wide_ref[...] = jnp.dot(h_ref[...].astype(bf16), out_ref[...], preferred_element_type=f32)
    send_sums("sum3", wide_ref[...], send3, recv3)
    part = queue_steps(6, 8, part)
    part_own[...] = jnp.sum(part, axis=0, keepdims=True)
    part_all[d] = part_own[...]
    column_peers("queue", part_own, part_all)
    send_norm("sum3", "norm3", recv3, own3, stat3)
    loads[5].wait()
    tables("norm3", stat3, channels)

    pooled = []
    for i in range(slots // 2):
        at = slice(2 * i * cells, (2 * i + 2) * cells)
        mean = jnp.concatenate([slot_row(mean_ref, 2 * i + o, channels) for o in range(2)], axis=0)
        scale = jnp.concatenate([slot_row(scale_ref, 2 * i + o, channels) for o in range(2)], axis=0)
        block = jax.nn.relu((wide_ref[at] - mean) * scale + x_ref[at].astype(f32)).astype(bf16)
        pooled.append(jnp.mean(block.astype(f32).reshape(2, cells, channels), axis=1))
    pooled = jnp.concatenate(pooled, axis=0).astype(bf16)
    z = jnp.dot(pooled, head_ref[...], preferred_element_type=f32)
    key_own[...] = (z * lax.rsqrt(jnp.sum(z * z, axis=-1, keepdims=True) + EPS_UNIT)).astype(bf16)
    key_all[d] = key_own[...]
    column_peers("key", key_own, key_all)

    arrived("queue", part_all)
    negative_all = jnp.sum(part_all[...], axis=0)
    mine = lax.broadcasted_iota(jnp.int32, (slots, n_dp * slots), 1) == (
        lax.broadcasted_iota(jnp.int32, (slots, n_dp * slots), 0) + d * slots
    )
    negative_col = jnp.sum(jnp.where(mine, negative_all, 0.0), axis=1, keepdims=True)
    negative = jnp.sum(jnp.where(lane == sub, negative_col, 0.0), axis=0, keepdims=True)
    want = (pos_row // (slots * n_bn)) * slots + pos_row % slots

    arrived("key", key_all)
    keys = key_all[...].reshape(n_dp * slots, key_all.shape[2])
    pairs = lax.dot_general(keys, query_own[...], (((1,), (1,)), ((), ())), preferred_element_type=f32)
    chosen = lax.broadcasted_iota(jnp.int32, pairs.shape, 0) == want
    logit = jnp.sum(jnp.where(chosen, pairs, 0.0), axis=0, keepdims=True) * INV_TEMP
    loss_ref[...] = jnp.log(jnp.exp(logit - INV_TEMP) + negative) + INV_TEMP - logit

    for phase, dst in zip(PHASES, (query_all, recv1, stat1, recv2, stat2, recv3, stat3, part_all, key_all)):
        sent(phase, dst)


def on_device_fixed(n_dp, n_bn, features, shuffle_masks, conv_in, conv_mid, conv_out, head, queries, queue, positive):
    f32, bf16 = jnp.float32, jnp.bfloat16
    slots, cells, channels = features.shape
    rows = slots * cells
    middle = conv_in.shape[1]
    width = queries.shape[1]
    n_dev = n_dp * n_bn

    def exchange(c):
        tile = (2 * (c // n_bn // LANES), LANES)
        return [
            pltpu.VMEM((n_dp, n_bn) + tile, f32),
            pltpu.VMEM((n_dev,) + tile, f32),
            pltpu.VMEM(tile, f32),
            pltpu.VMEM((n_dev,) + tile, f32),
        ]

    smem = pl.BlockSpec(memory_space=pltpu.SMEM)
    vmem = pl.BlockSpec(memory_space=pltpu.VMEM)
    hbm = pl.BlockSpec(memory_space=pl.ANY)
    loss = pl.pallas_call(
        functools.partial(fixed_kernel, n_dp, n_bn),
        out_shape=jax.ShapeDtypeStruct((1, slots), f32),
        in_specs=[smem, smem, vmem] + [hbm] * 6,
        out_specs=vmem,
        scratch_shapes=[
            pltpu.VMEM((rows, channels), bf16),
            pltpu.VMEM(conv_in.shape, bf16),
            pltpu.VMEM(conv_mid.shape, bf16),
            pltpu.VMEM(conv_out.shape, bf16),
            pltpu.VMEM(head.shape, bf16),
            pltpu.VMEM(queue.shape, bf16),
            pltpu.VMEM((rows, middle), f32),
            pltpu.VMEM((rows, channels), f32),
            pltpu.VMEM((n_dp, channels), f32),
            pltpu.VMEM((n_dp, channels), f32),
        ]
        + exchange(middle)
        + exchange(middle)
        + exchange(channels)
        + [
            pltpu.VMEM((slots, width), bf16),
            pltpu.VMEM((n_dp, slots, width), bf16),
            pltpu.VMEM((1, n_dp * slots), f32),
            pltpu.VMEM((n_dp, 1, n_dp * slots), f32),
            pltpu.VMEM((slots, width), bf16),
            pltpu.VMEM((n_dp, slots, width), bf16),
            pltpu.SemaphoreType.DMA((6,)),
            pltpu.SemaphoreType.DMA((len(PHASES),)),
            pltpu.SemaphoreType.DMA((len(PHASES),)),
        ],
        compiler_params=pltpu.CompilerParams(
            collective_id=0, has_side_effects=True, vmem_limit_bytes=48 << 20
        ),
        name="fixed_crops",
    )(shuffle_masks, positive, queries, features.reshape(rows, channels), conv_in, conv_mid, conv_out, head, queue)
    return loss.reshape(slots)


def on_device(n_dp, n_bn, *arrays):
    features, conv_in = arrays[0], arrays[2]
    whole_lanes = conv_in.shape[1] % (n_bn * LANES) == 0 and features.shape[2] % (n_bn * LANES) == 0
    if whole_lanes and n_dp <= features.shape[0] and features.shape[1] == 8:
        return on_device_fixed(n_dp, n_bn, *arrays)
    return on_device_moving(*arrays)


def solution(mesh):
    return jax.shard_map(
        functools.partial(on_device, mesh.shape["dp"], mesh.shape["bn"]),
        mesh=mesh,
        in_specs=(
            P(("dp", "bn"), None, None),
            P(),
            P(),
            P(),
            P(),
            P(),
            P(("dp", "bn"), None),
            P("dp", None),
            P(("dp", "bn")),
        ),
        out_specs=P(("dp", "bn")),
        check_vma=False,
    )
```

```python
import functools

import jax
import jax.numpy as jnp
from jax import lax
from jax.experimental import pallas as pl
from jax.experimental.pallas import tpu as pltpu
from jax.sharding import PartitionSpec as P

EPS_BN = 1e-05
EPS_UNIT = 1e-06
INV_TEMP = 1.0 / 0.07


def partner_2(value, axis, distance):
    return lax.ppermute(value, axis, [(i, i ^ 1 << distance) for i in range(lax.axis_size(axis))])


def unit_rows(values):
    values = values.astype(jnp.float32)
    return values * lax.rsqrt(jnp.sum(values * values, axis=-1, keepdims=True) + EPS_UNIT)


def group_norm(values, row_total):
    first = lax.psum(jnp.sum(values, axis=0), "bn")
    center = first / row_total
    spread = lax.psum(jnp.sum(jnp.square(values - center), axis=0), "bn") / row_total
    return (values - center) * lax.rsqrt(spread + EPS_BN)


def moving_slots(shuffle_masks, level, half):
    flags = jnp.bitwise_and(jnp.right_shift(shuffle_masks, level), 1)
    return jnp.argsort(1 - flags, stable=True)[:half]


def on_device_moving(features, shuffle_masks, conv_in, conv_mid, conv_out, head, queries, queue, positive):
    dp_count = lax.axis_size("dp")
    bn_count = lax.axis_size("bn")
    bit_count = dp_count.bit_length() - 1
    crop_dev, positions, channels = features.shape
    half = crop_dev // 2
    middle = conv_in.shape[1]
    query_unit = unit_rows(queries).astype(jnp.bfloat16)
    query_all = lax.all_gather(query_unit, "dp", axis=0, tiled=True)
    shuffled = features
    for level in range(bit_count):
        moving = moving_slots(shuffle_masks, level, half)
        partner = partner_2(jnp.take(shuffled, moving, axis=0), "dp", level)
        shuffled = shuffled.at[moving].set(partner)
    row_total = crop_dev * positions * bn_count
    flat_rows = shuffled.reshape(crop_dev * positions, channels)
    first_sum = jnp.dot(flat_rows, conv_in, preferred_element_type=jnp.float32)
    first_act = jax.nn.relu(group_norm(first_sum, row_total)).astype(jnp.bfloat16)
    tap_maps = first_act.reshape(crop_dev, positions, middle)
    padded = jnp.pad(tap_maps, ((0, 0), (1, 1), (0, 0)))
    stacked = jnp.concatenate([padded[:, tap : tap + positions, :] for tap in range(3)], axis=2)
    second_sum = jnp.dot(
        stacked.reshape(crop_dev * positions, 3 * middle),
        conv_mid.reshape(3 * middle, middle),
        preferred_element_type=jnp.float32,
    )
    second_act = jax.nn.relu(group_norm(second_sum, row_total)).astype(jnp.bfloat16)
    third_sum = jnp.dot(second_act, conv_out, preferred_element_type=jnp.float32)
    block = jax.nn.relu(group_norm(third_sum, row_total) + flat_rows.astype(jnp.float32)).astype(
        jnp.bfloat16
    )
    pooled = jnp.mean(
        block.reshape(crop_dev, positions, channels).astype(jnp.float32), axis=1
    ).astype(jnp.bfloat16)
    key_unit = unit_rows(jnp.dot(pooled, head, preferred_element_type=jnp.float32)).astype(
        jnp.bfloat16
    )
    for level in range(bit_count):
        moving = moving_slots(shuffle_masks, level, half)
        partner = partner_2(jnp.take(key_unit, moving, axis=0), "dp", level)
        key_unit = key_unit.at[moving].set(partner)
    queue_unit = unit_rows(queue).astype(jnp.bfloat16)
    scores = jnp.dot(query_all, queue_unit.T, preferred_element_type=jnp.float32) * INV_TEMP
    queue_part = jnp.sum(jnp.exp(scores - INV_TEMP), axis=1)
    key_all = lax.all_gather(key_unit, "dp", axis=0, tiled=True)
    slot_of = positive % crop_dev
    column = positive // crop_dev // bn_count
    picked = jnp.take(key_all, column * crop_dev + slot_of, axis=0)
    positive_logit = (
        jnp.sum(query_unit.astype(jnp.float32) * picked.astype(jnp.float32), axis=-1) * INV_TEMP
    )
    negative = lax.psum_scatter(queue_part, "dp", scatter_dimension=0, tiled=True)
    return jnp.log(jnp.exp(positive_logit - INV_TEMP) + negative) + INV_TEMP - positive_logit


MESH = pl.DeviceIdType.MESH
LANES = 128
QUEUE_STEPS = 8
PANELS = 4
PHASES = ("query", "sum1", "norm1", "sum2", "norm2", "sum3", "norm3", "queue", "key")


def fixed_kernel(
    n_dp, n_bn,
    masks_hbm, positive_hbm, queries_hbm, x_hbm, in_hbm, mid_hbm, out_hbm, head_hbm, queue_hbm,
    loss_ref,
    masks, positive, queries,
    x_ref, in_ref, mid_ref, out_ref, head_ref, queue_ref,
    h_ref, wide_ref, mean_ref, scale_ref,
    send1, recv1, own1, stat1, send2, recv2, own2, stat2, send3, recv3, own3, stat3,
    query_own, query_all, part_own, part_all, key_own, key_all,
    load_sem, panel_sem, send_sem, recv_sem,
):
    f32, bf16 = jnp.float32, jnp.bfloat16
    n_dev = n_dp * n_bn
    d = lax.axis_index("dp")
    b = lax.axis_index("bn")
    me = d * n_bn + b
    rows, channels = x_ref.shape
    slots = masks.shape[0]
    cells = rows // slots
    middle = in_ref.shape[1]
    total = float(rows * n_bn)

    panel = channels // PANELS
    panels = [
        pltpu.make_async_copy(
            in_hbm.at[pl.ds(i * panel, panel)], in_ref.at[pl.ds(i * panel, panel)], panel_sem.at[i]
        )
        for i in range(PANELS)
    ]
    loads = [
        pltpu.make_async_copy(src, dst, load_sem.at[i])
        for i, (src, dst) in enumerate(
            [(masks_hbm, masks), (positive_hbm, positive), (queries_hbm, queries), (x_hbm, x_ref), (queue_hbm, queue_ref), (mid_hbm, mid_ref), (out_hbm, out_ref), (head_hbm, head_ref)]
        )
    ]
    for load in loads[:4] + panels:
        load.start()

    barrier = pltpu.get_barrier_semaphore()

    dps = [lax.rem(d + k, n_dp) for k in range(n_dp)]
    bns = [lax.rem(b + k, n_bn) for k in range(n_bn)]
    peers = [(g, j) for g in dps for j in bns][1:]
    for peer in peers:
        pl.semaphore_signal(barrier, inc=1, device_id=peer, device_id_type=MESH)

    for load in loads[:3]:
        load.wait()
    lane = lax.broadcasted_iota(jnp.int32, (slots, slots), 1)
    sub = lax.broadcasted_iota(jnp.int32, (slots, slots), 0)
    mask_row = jnp.zeros((slots, slots), jnp.int32)
    mask_col = jnp.zeros((slots, slots), jnp.int32)
    pos_row = jnp.zeros((1, slots), jnp.int32)
    lane1 = lax.broadcasted_iota(jnp.int32, (1, slots), 1)
    groups = []
    for s in range(slots):
        groups.append(masks[s] ^ d)
        mask_row = jnp.where(lane == s, groups[s], mask_row)
        mask_col = jnp.where(sub == s, groups[s], mask_col)
        pos_row = jnp.where(lane1 == s, positive[s], pos_row)
    same = (mask_row == mask_col).astype(f32)
    local_mean = same / (jnp.sum(same, axis=0, keepdims=True) * float(cells))
    member = (mask_row[:n_dp] == sub[:n_dp]).astype(f32) if n_dp <= slots else None
    counts = []
    for e in range(n_dp):
        want = e ^ d
        count = jnp.int32(0)
        for s in range(slots):
            count = count + (masks[s] == want).astype(jnp.int32)
        counts.append((count * cells).astype(f32))

    q = queries[...].astype(f32)
    query_unit = (q * lax.rsqrt(jnp.sum(q * q, axis=-1, keepdims=True) + EPS_UNIT)).astype(bf16)
    query_own[...] = query_unit
    query_all[d] = query_unit

    def all_peers(phase, src_of, dst):
        i = PHASES.index(phase)

        for g, j in peers:
            pltpu.make_async_remote_copy(
                src_ref=src_of(g, j), dst_ref=dst.at[me],
                send_sem=send_sem.at[i], recv_sem=recv_sem.at[i],
                device_id=(g, j), device_id_type=MESH,
            ).start()

    def column_peers(phase, src, dst):
        i = PHASES.index(phase)

        for g in dps[1:]:
            pltpu.make_async_remote_copy(
                src_ref=src, dst_ref=dst.at[d],
                send_sem=send_sem.at[i], recv_sem=recv_sem.at[i],
                device_id=(g, b), device_id_type=MESH,
            ).start()

    def arrived(phase, dst):
        most = dst.at[pl.ds(0, dst.shape[0] - 1)]
        pltpu.make_async_copy(most, most, recv_sem.at[PHASES.index(phase)]).wait()

    def sent(phase, dst):
        most = dst.at[pl.ds(0, dst.shape[0] - 1)]
        pltpu.make_async_copy(most, most, send_sem.at[PHASES.index(phase)]).wait()

    def exact(a, c):
        return jnp.dot(a, c, preferred_element_type=f32, precision=lax.Precision.HIGHEST)

    def send_sums(phase, h, send, recv):
        width = h.shape[1]
        block = width // n_bn
        subs = block // LANES
        shaped = h.reshape(slots, cells, width)
        sums = jnp.sum(shaped, axis=1)
        center = exact(local_mean, sums)
        squares = jnp.sum(jnp.square(shaped - center[:, None, :]), axis=1)
        for at, values in ((0, exact(member, sums)), (subs, exact(member, squares))):
            for j in range(n_bn):
                for r in range(subs):
                    low = j * block + r * LANES
                    send[:, j, at + r, :] = values[:, low : low + LANES]
        recv[me] = send[d, b]
        all_peers(phase, lambda g, j: send.at[g, j], recv)

    def send_norm(phase_in, phase_out, recv, own, stat):
        arrived(phase_in, recv)
        subs = recv.shape[1] // 2
        both = jnp.sum(recv[...], axis=0)
        mean = both[:subs] * (1.0 / total)
        spread = both[subs:]
        for e in range(n_dp):
            part = recv[e * n_bn : (e + 1) * n_bn][:, :subs]
            off = jnp.sum(jnp.square(part - counts[e] * mean[None]), axis=0)
            spread = spread + off / jnp.maximum(counts[e], 1.0)
        own[:subs] = mean
        own[subs:] = lax.rsqrt(spread * (1.0 / total) + EPS_BN)
        stat[me] = own[...]
        all_peers(phase_out, lambda g, j: own, stat)

    def tables(phase, stat, width):
        arrived(phase, stat)
        block = width // n_bn
        subs = block // LANES
        held = stat[...].reshape(n_dp, n_bn, 2 * subs, LANES)
        for j in range(n_bn):
            for r in range(subs):
                low = j * block + r * LANES
                mean_ref[:, low : low + LANES] = held[:, j, r, :]
                scale_ref[:, low : low + LANES] = held[:, j, subs + r, :]

    def slot_row(table, s, width):
        return jnp.broadcast_to(table[pl.ds(groups[s], 1), :width], (cells, width))

    ones = jnp.ones((LANES, LANES), bf16)
    step_rows = queue_ref.shape[0] // QUEUE_STEPS

    def queue_step(c, total_part):
        raw = queue_ref[pl.ds(c * step_rows, step_rows), :].astype(f32)
        square = raw * raw
        high = square.astype(bf16)
        low = (square - high.astype(f32)).astype(bf16)
        norm = jnp.dot(high, ones, preferred_element_type=f32) + jnp.dot(low, ones, preferred_element_type=f32)
        unit = (raw * lax.rsqrt(norm + EPS_UNIT)).astype(bf16)
        flat_queries = query_all[...].reshape(n_dp * slots, query_all.shape[2])
        scores = lax.dot_general(unit, flat_queries, (((1,), (1,)), ((), ())), preferred_element_type=f32)
        terms = jnp.exp(scores * INV_TEMP - INV_TEMP)
        return total_part + jnp.sum(terms.reshape(step_rows // 8, 8, n_dp * slots), axis=0)

    def queue_steps(first, last, total_part):
        return lax.fori_loop(first, last, queue_step, total_part)

    loads[3].wait()
    first = None
    for i in range(PANELS):
        panels[i].wait()
        at = slice(i * panel, (i + 1) * panel)
        term = jnp.dot(x_ref[:, at], in_ref[at], preferred_element_type=f32)
        first = term if first is None else first + term
        if i == 0:
            for load in loads[4:]:
                load.start()
    h_ref[...] = first
    pl.semaphore_wait(barrier, n_dev - 1)
    column_peers("query", query_own, query_all)
    send_sums("sum1", h_ref[...], send1, recv1)
    part = jnp.zeros((8, n_dp * slots), f32)
    loads[4].wait()
    arrived("query", query_all)
    part = queue_steps(0, 2, part)
    send_norm("sum1", "norm1", recv1, own1, stat1)
    loads[5].wait()
    part = queue_steps(2, 3, part)
    tables("norm1", stat1, middle)

    for s in range(slots):
        at = slice(s * cells, (s + 1) * cells)
        h_ref[at] = jax.nn.relu((h_ref[at] - slot_row(mean_ref, s, middle)) * slot_row(scale_ref, s, middle))
    act = h_ref[...]
    cell = lax.broadcasted_iota(jnp.int32, act.shape, 0) % cells
    before = jnp.where(cell == 0, 0.0, pltpu.roll(act, 1, 0)).astype(bf16)
    after = jnp.where(cell == cells - 1, 0.0, pltpu.roll(act, rows - 1, 0)).astype(bf16)
    h_ref[...] = (
        jnp.dot(before, mid_ref[0], preferred_element_type=f32)
        + jnp.dot(act.astype(bf16), mid_ref[1], preferred_element_type=f32)
        + jnp.dot(after, mid_ref[2], preferred_element_type=f32)
    )
    send_sums("sum2", h_ref[...], send2, recv2)
    part = queue_steps(3, 5, part)
    send_norm("sum2", "norm2", recv2, own2, stat2)
    loads[6].wait()
    part = queue_steps(5, 6, part)
    tables("norm2", stat2, middle)

    for s in range(slots):
        at = slice(s * cells, (s + 1) * cells)
        h_ref[at] = jax.nn.relu((h_ref[at] - slot_row(mean_ref, s, middle)) * slot_row(scale_ref, s, middle))
    wide_ref[...] = jnp.dot(h_ref[...].astype(bf16), out_ref[...], preferred_element_type=f32)
    send_sums("sum3", wide_ref[...], send3, recv3)
    part = queue_steps(6, 8, part)
    part_own[...] = jnp.sum(part, axis=0, keepdims=True)
    part_all[d] = part_own[...]
    column_peers("queue", part_own, part_all)
    send_norm("sum3", "norm3", recv3, own3, stat3)
    loads[7].wait()
    tables("norm3", stat3, channels)

    pooled = []
    for i in range(slots // 2):
        at = slice(2 * i * cells, (2 * i + 2) * cells)
        mean = jnp.concatenate([slot_row(mean_ref, 2 * i + o, channels) for o in range(2)], axis=0)
        scale = jnp.concatenate([slot_row(scale_ref, 2 * i + o, channels) for o in range(2)], axis=0)
        block = jax.nn.relu((wide_ref[at] - mean) * scale + x_ref[at].astype(f32)).astype(bf16)
        pooled.append(jnp.mean(block.astype(f32).reshape(2, cells, channels), axis=1))
    pooled = jnp.concatenate(pooled, axis=0).astype(bf16)
    z = jnp.dot(pooled, head_ref[...], preferred_element_type=f32)
    key_own[...] = (z * lax.rsqrt(jnp.sum(z * z, axis=-1, keepdims=True) + EPS_UNIT)).astype(bf16)
    key_all[d] = key_own[...]
    column_peers("key", key_own, key_all)

    arrived("queue", part_all)
    negative_all = jnp.sum(part_all[...], axis=0)
    mine = lax.broadcasted_iota(jnp.int32, (slots, n_dp * slots), 1) == (
        lax.broadcasted_iota(jnp.int32, (slots, n_dp * slots), 0) + d * slots
    )
    negative_col = jnp.sum(jnp.where(mine, negative_all, 0.0), axis=1, keepdims=True)
    negative = jnp.sum(jnp.where(lane == sub, negative_col, 0.0), axis=0, keepdims=True)
    want = (pos_row // (slots * n_bn)) * slots + pos_row % slots

    arrived("key", key_all)
    keys = key_all[...].reshape(n_dp * slots, key_all.shape[2])
    pairs = lax.dot_general(keys, query_own[...], (((1,), (1,)), ((), ())), preferred_element_type=f32)
    chosen = lax.broadcasted_iota(jnp.int32, pairs.shape, 0) == want
    logit = jnp.sum(jnp.where(chosen, pairs, 0.0), axis=0, keepdims=True) * INV_TEMP
    loss_ref[...] = jnp.log(jnp.exp(logit - INV_TEMP) + negative) + INV_TEMP - logit

    for phase, dst in zip(PHASES, (query_all, recv1, stat1, recv2, stat2, recv3, stat3, part_all, key_all)):
        sent(phase, dst)


def on_device_fixed(n_dp, n_bn, features, shuffle_masks, conv_in, conv_mid, conv_out, head, queries, queue, positive):
    f32, bf16 = jnp.float32, jnp.bfloat16
    slots, cells, channels = features.shape
    rows = slots * cells
    middle = conv_in.shape[1]
    width = queries.shape[1]
    n_dev = n_dp * n_bn

    def exchange(c):
        tile = (2 * (c // n_bn // LANES), LANES)
        return [
            pltpu.VMEM((n_dp, n_bn) + tile, f32),
            pltpu.VMEM((n_dev,) + tile, f32),
            pltpu.VMEM(tile, f32),
            pltpu.VMEM((n_dev,) + tile, f32),
        ]

    vmem = pl.BlockSpec(memory_space=pltpu.VMEM)
    hbm = pl.BlockSpec(memory_space=pltpu.HBM)
    loss = pl.pallas_call(
        functools.partial(fixed_kernel, n_dp, n_bn),
        out_shape=jax.ShapeDtypeStruct((1, slots), f32),
        in_specs=[hbm] * 9,
        out_specs=vmem,
        scratch_shapes=[
            pltpu.SMEM(shuffle_masks.shape, jnp.int32),
            pltpu.SMEM(positive.shape, jnp.int32),
            pltpu.VMEM(queries.shape, bf16),
            pltpu.VMEM((rows, channels), bf16),
            pltpu.VMEM(conv_in.shape, bf16),
            pltpu.VMEM(conv_mid.shape, bf16),
            pltpu.VMEM(conv_out.shape, bf16),
            pltpu.VMEM(head.shape, bf16),
            pltpu.VMEM(queue.shape, bf16),
            pltpu.VMEM((rows, middle), f32),
            pltpu.VMEM((rows, channels), f32),
            pltpu.VMEM((n_dp, channels), f32),
            pltpu.VMEM((n_dp, channels), f32),
        ]
        + exchange(middle)
        + exchange(middle)
        + exchange(channels)
        + [
            pltpu.VMEM((slots, width), bf16),
            pltpu.VMEM((n_dp, slots, width), bf16),
            pltpu.VMEM((1, n_dp * slots), f32),
            pltpu.VMEM((n_dp, 1, n_dp * slots), f32),
            pltpu.VMEM((slots, width), bf16),
            pltpu.VMEM((n_dp, slots, width), bf16),
            pltpu.SemaphoreType.DMA((8,)),
            pltpu.SemaphoreType.DMA((PANELS,)),
            pltpu.SemaphoreType.DMA((len(PHASES),)),
            pltpu.SemaphoreType.DMA((len(PHASES),)),
        ],
        compiler_params=pltpu.CompilerParams(
            collective_id=0, has_side_effects=True, vmem_limit_bytes=64 << 20
        ),
        name="fixed_crops",
    )(shuffle_masks, positive, queries, features.reshape(rows, channels), conv_in, conv_mid, conv_out, head, queue)
    return loss.reshape(slots)


def on_device(n_dp, n_bn, *arrays):
    features, conv_in = arrays[0], arrays[2]
    whole_lanes = conv_in.shape[1] % (n_bn * LANES) == 0 and features.shape[2] % (n_bn * LANES) == 0
    if whole_lanes and n_dp <= features.shape[0] and features.shape[1] == 8:
        return on_device_fixed(n_dp, n_bn, *arrays)
    return on_device_moving(*arrays)


def solution(mesh):
    return jax.shard_map(
        functools.partial(on_device, mesh.shape["dp"], mesh.shape["bn"]),
        mesh=mesh,
        in_specs=(
            P(("dp", "bn"), None, None),
            P(),
            P(),
            P(),
            P(),
            P(),
            P(("dp", "bn"), None),
            P("dp", None),
            P(("dp", "bn")),
        ),
        out_specs=P(("dp", "bn")),
        check_vma=False,
    )
```

```python
import functools

import jax
import jax.numpy as jnp
from jax import lax
from jax.experimental import pallas as pl
from jax.experimental.pallas import tpu as pltpu
from jax.sharding import PartitionSpec as P

EPS_BN = 1e-05
EPS_UNIT = 1e-06
INV_TEMP = 1.0 / 0.07


def partner_2(value, axis, distance):
    return lax.ppermute(value, axis, [(i, i ^ 1 << distance) for i in range(lax.axis_size(axis))])


def unit_rows(values):
    values = values.astype(jnp.float32)
    return values * lax.rsqrt(jnp.sum(values * values, axis=-1, keepdims=True) + EPS_UNIT)


def group_norm(values, row_total):
    first = lax.psum(jnp.sum(values, axis=0), "bn")
    center = first / row_total
    spread = lax.psum(jnp.sum(jnp.square(values - center), axis=0), "bn") / row_total
    return (values - center) * lax.rsqrt(spread + EPS_BN)


def moving_slots(shuffle_masks, level, half):
    flags = jnp.bitwise_and(jnp.right_shift(shuffle_masks, level), 1)
    return jnp.argsort(1 - flags, stable=True)[:half]


def on_device_moving(features, shuffle_masks, conv_in, conv_mid, conv_out, head, queries, queue, positive):
    dp_count = lax.axis_size("dp")
    bn_count = lax.axis_size("bn")
    bit_count = dp_count.bit_length() - 1
    crop_dev, positions, channels = features.shape
    half = crop_dev // 2
    middle = conv_in.shape[1]
    query_unit = unit_rows(queries).astype(jnp.bfloat16)
    query_all = lax.all_gather(query_unit, "dp", axis=0, tiled=True)
    shuffled = features
    for level in range(bit_count):
        moving = moving_slots(shuffle_masks, level, half)
        partner = partner_2(jnp.take(shuffled, moving, axis=0), "dp", level)
        shuffled = shuffled.at[moving].set(partner)
    row_total = crop_dev * positions * bn_count
    flat_rows = shuffled.reshape(crop_dev * positions, channels)
    first_sum = jnp.dot(flat_rows, conv_in, preferred_element_type=jnp.float32)
    first_act = jax.nn.relu(group_norm(first_sum, row_total)).astype(jnp.bfloat16)
    tap_maps = first_act.reshape(crop_dev, positions, middle)
    padded = jnp.pad(tap_maps, ((0, 0), (1, 1), (0, 0)))
    stacked = jnp.concatenate([padded[:, tap : tap + positions, :] for tap in range(3)], axis=2)
    second_sum = jnp.dot(
        stacked.reshape(crop_dev * positions, 3 * middle),
        conv_mid.reshape(3 * middle, middle),
        preferred_element_type=jnp.float32,
    )
    second_act = jax.nn.relu(group_norm(second_sum, row_total)).astype(jnp.bfloat16)
    third_sum = jnp.dot(second_act, conv_out, preferred_element_type=jnp.float32)
    block = jax.nn.relu(group_norm(third_sum, row_total) + flat_rows.astype(jnp.float32)).astype(
        jnp.bfloat16
    )
    pooled = jnp.mean(
        block.reshape(crop_dev, positions, channels).astype(jnp.float32), axis=1
    ).astype(jnp.bfloat16)
    key_unit = unit_rows(jnp.dot(pooled, head, preferred_element_type=jnp.float32)).astype(
        jnp.bfloat16
    )
    for level in range(bit_count):
        moving = moving_slots(shuffle_masks, level, half)
        partner = partner_2(jnp.take(key_unit, moving, axis=0), "dp", level)
        key_unit = key_unit.at[moving].set(partner)
    queue_unit = unit_rows(queue).astype(jnp.bfloat16)
    scores = jnp.dot(query_all, queue_unit.T, preferred_element_type=jnp.float32) * INV_TEMP
    queue_part = jnp.sum(jnp.exp(scores - INV_TEMP), axis=1)
    key_all = lax.all_gather(key_unit, "dp", axis=0, tiled=True)
    slot_of = positive % crop_dev
    column = positive // crop_dev // bn_count
    picked = jnp.take(key_all, column * crop_dev + slot_of, axis=0)
    positive_logit = (
        jnp.sum(query_unit.astype(jnp.float32) * picked.astype(jnp.float32), axis=-1) * INV_TEMP
    )
    negative = lax.psum_scatter(queue_part, "dp", scatter_dimension=0, tiled=True)
    return jnp.log(jnp.exp(positive_logit - INV_TEMP) + negative) + INV_TEMP - positive_logit


MESH = pl.DeviceIdType.MESH
LANES = 128
QUEUE_STEPS = 8
PANELS = 4
PHASES = ("query", "sum1", "norm1", "sum2", "norm2", "sum3", "norm3", "queue", "key")


def fixed_kernel(
    n_dp, n_bn,
    masks_hbm, positive_hbm, queries_hbm, x_hbm, in_hbm, mid_hbm, out_hbm, head_hbm, queue_hbm,
    loss_ref,
    masks, positive, queries,
    x_ref, in_ref, mid_ref, out_ref, head_ref, queue_ref,
    h_ref, wide_ref, mean_ref, scale_ref,
    send1, recv1, own1, stat1, send2, recv2, own2, stat2, send3, recv3, own3, stat3,
    query_own, query_all, part_own, part_all, key_own, key_all,
    load_sem, panel_sem, send_sem, recv_sem, ready_sem,
):
    f32, bf16 = jnp.float32, jnp.bfloat16
    n_dev = n_dp * n_bn
    d = lax.axis_index("dp")
    b = lax.axis_index("bn")
    me = d * n_bn + b
    rows, channels = x_ref.shape
    slots = masks.shape[0]
    cells = rows // slots
    middle = in_ref.shape[1]
    total = float(rows * n_bn)

    panel = channels // PANELS
    panels = [
        pltpu.make_async_copy(
            in_hbm.at[pl.ds(i * panel, panel)], in_ref.at[pl.ds(i * panel, panel)], panel_sem.at[i]
        )
        for i in range(PANELS)
    ]
    loads = [
        pltpu.make_async_copy(src, dst, load_sem.at[i])
        for i, (src, dst) in enumerate(
            [(masks_hbm, masks), (positive_hbm, positive), (queries_hbm, queries), (x_hbm, x_ref), (queue_hbm, queue_ref), (mid_hbm, mid_ref), (out_hbm, out_ref), (head_hbm, head_ref)]
        )
    ]
    for load in loads[:4] + panels:
        load.start()

    barrier = pltpu.get_barrier_semaphore()

    dps = [lax.rem(d + k, n_dp) for k in range(n_dp)]
    bns = [lax.rem(b + k, n_bn) for k in range(n_bn)]
    order = [k for k in (n_dp // 2 + i * o for i in range(n_dp // 2) for o in (1, -1))]
    order = list(dict.fromkeys(order + list(range(n_dp))))
    peers = [(dps[k % n_dp], j) for k in order if k % n_dp for j in bns] + [(d, j) for j in bns[1:]]
    for peer in [(g, b) for g in dps[1:]] + [(d, j) for j in bns[1:]]:
        pl.semaphore_signal(barrier, inc=1, device_id=peer, device_id_type=MESH)

    n_own = n_dev // 2
    base = n_own // 2
    owner = jnp.logical_and(me >= base, me < base + n_own)
    mine_at = jnp.clip(me - base, 0, n_own - 1)

    for load in loads[:3]:
        load.wait()
    lane = lax.broadcasted_iota(jnp.int32, (slots, slots), 1)
    sub = lax.broadcasted_iota(jnp.int32, (slots, slots), 0)
    mask_row = jnp.zeros((slots, slots), jnp.int32)
    mask_col = jnp.zeros((slots, slots), jnp.int32)
    pos_row = jnp.zeros((1, slots), jnp.int32)
    lane1 = lax.broadcasted_iota(jnp.int32, (1, slots), 1)
    groups = []
    for s in range(slots):
        groups.append(masks[s] ^ d)
        mask_row = jnp.where(lane == s, groups[s], mask_row)
        mask_col = jnp.where(sub == s, groups[s], mask_col)
        pos_row = jnp.where(lane1 == s, positive[s], pos_row)
    same = (mask_row == mask_col).astype(f32)
    local_mean = same / (jnp.sum(same, axis=0, keepdims=True) * float(cells))
    member = (mask_row[:n_dp] == sub[:n_dp]).astype(f32) if n_dp <= slots else None
    counts = []
    for e in range(n_dp):
        want = e ^ lax.div(2 * mine_at, n_bn)
        count = jnp.int32(0)
        for s in range(slots):
            count = count + (masks[s] == want).astype(jnp.int32)
        counts.append((count * cells).astype(f32))

    q = queries[...].astype(f32)
    query_unit = (q * lax.rsqrt(jnp.sum(q * q, axis=-1, keepdims=True) + EPS_UNIT)).astype(bf16)
    query_own[...] = query_unit
    query_all[d] = query_unit

    def push(phase, src, dst, peer):
        i = PHASES.index(phase)
        pltpu.make_async_remote_copy(
            src_ref=src, dst_ref=dst, send_sem=send_sem.at[i], recv_sem=recv_sem.at[i],
            device_id=peer, device_id_type=MESH,
        ).start()

    def to_owners(phase, send, recv):
        for k in range(1, n_own + 1):
            o = lax.rem(me + k, n_own)
            t = o + base
            peer = (lax.div(t, n_bn), lax.rem(t, n_bn))
            if k == n_own - base:
                @pl.when(jnp.logical_not(owner))
                def _():
                    push(phase, send.at[o], recv.at[me], peer)
            else:
                push(phase, send.at[o], recv.at[me], peer)

        @pl.when(owner)
        def _():
            recv[me] = send[mine_at]

    def took(sem, ref, n):
        most = ref.at[pl.ds(0, n)]
        pltpu.make_async_copy(most, most, sem).wait()

    def took_owners(sem, ref):
        @pl.when(owner)
        def _():
            took(sem, ref, n_own - 1)

        @pl.when(jnp.logical_not(owner))
        def _():
            took(sem, ref, n_own)

    def column_peers(phase, src, dst):
        i = PHASES.index(phase)

        for g in dps[1:]:
            pltpu.make_async_remote_copy(
                src_ref=src, dst_ref=dst.at[d],
                send_sem=send_sem.at[i], recv_sem=recv_sem.at[i],
                device_id=(g, b), device_id_type=MESH,
            ).start()

    def arrived(phase, dst):
        most = dst.at[pl.ds(0, dst.shape[0] - 1)]
        pltpu.make_async_copy(most, most, recv_sem.at[PHASES.index(phase)]).wait()

    def sent(phase, dst):
        most = dst.at[pl.ds(0, dst.shape[0] - 1)]
        pltpu.make_async_copy(most, most, send_sem.at[PHASES.index(phase)]).wait()

    def exact(a, c):
        return jnp.dot(a, c, preferred_element_type=f32, precision=lax.Precision.HIGHEST)

    def send_sums(phase, h, send, recv):
        width = h.shape[1]
        block = width // n_bn
        subs = block // LANES
        shaped = h.reshape(slots, cells, width)
        sums = jnp.sum(shaped, axis=1)
        center = exact(local_mean, sums)
        squares = jnp.sum(jnp.square(shaped - center[:, None, :]), axis=1)
        for at, values in ((0, exact(member, sums)), (subs, exact(member, squares))):
            for j in range(n_bn):
                for r in range(subs):
                    low = j * block + r * LANES
                    block_rows = values[:, low : low + LANES]
                    for g in range(n_dp):
                        flat = g * n_bn + j
                        send[flat // 2, flat % 2, at + r, :] = block_rows[g]
        to_owners(phase, send, recv)

    def send_norm(phase_in, phase_out, recv, own, stat):
        @pl.when(owner)
        def _():
            took(recv_sem.at[PHASES.index(phase_in)], recv, n_dev - 1)
            subs = recv.shape[2] // 2
            both = jnp.sum(recv[...], axis=0)
            mean = both[:, :subs] * (1.0 / total)
            spread = both[:, subs:]
            for e in range(n_dp):
                part = recv[e * n_bn : (e + 1) * n_bn][:, :, :subs]
                off = jnp.sum(jnp.square(part - counts[e] * mean[None]), axis=0)
                spread = spread + off / jnp.maximum(counts[e], 1.0)
            own[:, :subs] = mean
            own[:, subs:] = lax.rsqrt(spread * (1.0 / total) + EPS_BN)
            stat[mine_at] = own[...]
            for peer in peers:
                push(phase_out, own, stat.at[mine_at], peer)

    def tables(phase, stat, width):
        took_owners(recv_sem.at[PHASES.index(phase)], stat)
        block = width // n_bn
        subs = block // LANES
        held = stat[...].reshape(n_dp, n_bn, 2 * subs, LANES)
        for j in range(n_bn):
            for r in range(subs):
                low = j * block + r * LANES
                mean_ref[:, low : low + LANES] = held[:, j, r, :]
                scale_ref[:, low : low + LANES] = held[:, j, subs + r, :]

    def slot_row(table, s, width):
        return jnp.broadcast_to(table[pl.ds(groups[s], 1), :width], (cells, width))

    ones = jnp.ones((LANES, LANES), bf16)
    step_rows = queue_ref.shape[0] // QUEUE_STEPS

    def queue_step(c, total_part):
        raw = queue_ref[pl.ds(c * step_rows, step_rows), :].astype(f32)
        square = raw * raw
        high = square.astype(bf16)
        low = (square - high.astype(f32)).astype(bf16)
        norm = jnp.dot(high, ones, preferred_element_type=f32) + jnp.dot(low, ones, preferred_element_type=f32)
        unit = (raw * lax.rsqrt(norm + EPS_UNIT)).astype(bf16)
        flat_queries = query_all[...].reshape(n_dp * slots, query_all.shape[2])
        scores = lax.dot_general(unit, flat_queries, (((1,), (1,)), ((), ())), preferred_element_type=f32)
        terms = jnp.exp(scores * INV_TEMP - INV_TEMP)
        return total_part + jnp.sum(terms.reshape(step_rows // 8, 8, n_dp * slots), axis=0)

    def queue_steps(first, last, total_part):
        return lax.fori_loop(first, last, queue_step, total_part)

    loads[3].wait()
    first = None
    for i in range(PANELS):
        panels[i].wait()
        at = slice(i * panel, (i + 1) * panel)
        term = jnp.dot(x_ref[:, at], in_ref[at], preferred_element_type=f32)
        first = term if first is None else first + term
        if i == 0:
            for load in loads[4:]:
                load.start()
            pl.semaphore_wait(barrier, n_dp + n_bn - 2)
            for j in bns[1:]:
                pl.semaphore_signal(ready_sem, inc=1, device_id=(d, j), device_id_type=MESH)
    h_ref[...] = first
    pl.semaphore_wait(ready_sem, n_bn - 1)
    column_peers("query", query_own, query_all)
    send_sums("sum1", h_ref[...], send1, recv1)
    part = jnp.zeros((8, n_dp * slots), f32)
    loads[4].wait()
    arrived("query", query_all)
    part = queue_steps(0, 2, part)
    send_norm("sum1", "norm1", recv1, own1, stat1)
    loads[5].wait()
    part = queue_steps(2, 3, part)
    tables("norm1", stat1, middle)

    for s in range(slots):
        at = slice(s * cells, (s + 1) * cells)
        h_ref[at] = jax.nn.relu((h_ref[at] - slot_row(mean_ref, s, middle)) * slot_row(scale_ref, s, middle))
    act = h_ref[...]
    cell = lax.broadcasted_iota(jnp.int32, act.shape, 0) % cells
    before = jnp.where(cell == 0, 0.0, pltpu.roll(act, 1, 0)).astype(bf16)
    after = jnp.where(cell == cells - 1, 0.0, pltpu.roll(act, rows - 1, 0)).astype(bf16)
    h_ref[...] = (
        jnp.dot(before, mid_ref[0], preferred_element_type=f32)
        + jnp.dot(act.astype(bf16), mid_ref[1], preferred_element_type=f32)
        + jnp.dot(after, mid_ref[2], preferred_element_type=f32)
    )
    send_sums("sum2", h_ref[...], send2, recv2)
    part = queue_steps(3, 5, part)
    send_norm("sum2", "norm2", recv2, own2, stat2)
    loads[6].wait()
    part = queue_steps(5, 6, part)
    tables("norm2", stat2, middle)

    for s in range(slots):
        at = slice(s * cells, (s + 1) * cells)
        h_ref[at] = jax.nn.relu((h_ref[at] - slot_row(mean_ref, s, middle)) * slot_row(scale_ref, s, middle))
    wide_ref[...] = jnp.dot(h_ref[...].astype(bf16), out_ref[...], preferred_element_type=f32)
    send_sums("sum3", wide_ref[...], send3, recv3)
    part = queue_steps(6, 8, part)
    part_own[...] = jnp.sum(part, axis=0, keepdims=True)
    part_all[d] = part_own[...]
    column_peers("queue", part_own, part_all)
    send_norm("sum3", "norm3", recv3, own3, stat3)
    loads[7].wait()
    tables("norm3", stat3, channels)

    pooled = []
    for i in range(slots // 2):
        at = slice(2 * i * cells, (2 * i + 2) * cells)
        mean = jnp.concatenate([slot_row(mean_ref, 2 * i + o, channels) for o in range(2)], axis=0)
        scale = jnp.concatenate([slot_row(scale_ref, 2 * i + o, channels) for o in range(2)], axis=0)
        block = jax.nn.relu((wide_ref[at] - mean) * scale + x_ref[at].astype(f32)).astype(bf16)
        pooled.append(jnp.mean(block.astype(f32).reshape(2, cells, channels), axis=1))
    pooled = jnp.concatenate(pooled, axis=0).astype(bf16)
    z = jnp.dot(pooled, head_ref[...], preferred_element_type=f32)
    key_own[...] = (z * lax.rsqrt(jnp.sum(z * z, axis=-1, keepdims=True) + EPS_UNIT)).astype(bf16)
    key_all[d] = key_own[...]
    column_peers("key", key_own, key_all)

    arrived("queue", part_all)
    negative_all = jnp.sum(part_all[...], axis=0)
    mine = lax.broadcasted_iota(jnp.int32, (slots, n_dp * slots), 1) == (
        lax.broadcasted_iota(jnp.int32, (slots, n_dp * slots), 0) + d * slots
    )
    negative_col = jnp.sum(jnp.where(mine, negative_all, 0.0), axis=1, keepdims=True)
    negative = jnp.sum(jnp.where(lane == sub, negative_col, 0.0), axis=0, keepdims=True)
    want = (pos_row // (slots * n_bn)) * slots + pos_row % slots

    arrived("key", key_all)
    keys = key_all[...].reshape(n_dp * slots, key_all.shape[2])
    pairs = lax.dot_general(keys, query_own[...], (((1,), (1,)), ((), ())), preferred_element_type=f32)
    chosen = lax.broadcasted_iota(jnp.int32, pairs.shape, 0) == want
    logit = jnp.sum(jnp.where(chosen, pairs, 0.0), axis=0, keepdims=True) * INV_TEMP
    loss_ref[...] = jnp.log(jnp.exp(logit - INV_TEMP) + negative) + INV_TEMP - logit

    for phase, dst in (("query", query_all), ("queue", part_all), ("key", key_all)):
        sent(phase, dst)
    for i, send, recv in ((1, send1, recv1), (3, send2, recv2), (5, send3, recv3)):
        took_owners(send_sem.at[i], send)

        @pl.when(owner)
        def _():
            took(send_sem.at[i + 1], recv, n_dev - 1)


def on_device_fixed(n_dp, n_bn, features, shuffle_masks, conv_in, conv_mid, conv_out, head, queries, queue, positive):
    f32, bf16 = jnp.float32, jnp.bfloat16
    slots, cells, channels = features.shape
    rows = slots * cells
    middle = conv_in.shape[1]
    width = queries.shape[1]
    n_dev = n_dp * n_bn

    def exchange(c):
        tile = (2 * (c // n_bn // LANES), LANES)
        return [
            pltpu.VMEM((n_dev // 2, 2) + tile, f32),
            pltpu.VMEM((n_dev, 2) + tile, f32),
            pltpu.VMEM((2,) + tile, f32),
            pltpu.VMEM((n_dev // 2, 2) + tile, f32),
        ]

    vmem = pl.BlockSpec(memory_space=pltpu.VMEM)
    hbm = pl.BlockSpec(memory_space=pltpu.HBM)
    loss = pl.pallas_call(
        functools.partial(fixed_kernel, n_dp, n_bn),
        out_shape=jax.ShapeDtypeStruct((1, slots), f32),
        in_specs=[hbm] * 9,
        out_specs=vmem,
        scratch_shapes=[
            pltpu.SMEM(shuffle_masks.shape, jnp.int32),
            pltpu.SMEM(positive.shape, jnp.int32),
            pltpu.VMEM(queries.shape, bf16),
            pltpu.VMEM((rows, channels), bf16),
            pltpu.VMEM(conv_in.shape, bf16),
            pltpu.VMEM(conv_mid.shape, bf16),
            pltpu.VMEM(conv_out.shape, bf16),
            pltpu.VMEM(head.shape, bf16),
            pltpu.VMEM(queue.shape, bf16),
            pltpu.VMEM((rows, middle), f32),
            pltpu.VMEM((rows, channels), f32),
            pltpu.VMEM((n_dp, channels), f32),
            pltpu.VMEM((n_dp, channels), f32),
        ]
        + exchange(middle)
        + exchange(middle)
        + exchange(channels)
        + [
            pltpu.VMEM((slots, width), bf16),
            pltpu.VMEM((n_dp, slots, width), bf16),
            pltpu.VMEM((1, n_dp * slots), f32),
            pltpu.VMEM((n_dp, 1, n_dp * slots), f32),
            pltpu.VMEM((slots, width), bf16),
            pltpu.VMEM((n_dp, slots, width), bf16),
            pltpu.SemaphoreType.DMA((8,)),
            pltpu.SemaphoreType.DMA((PANELS,)),
            pltpu.SemaphoreType.DMA((len(PHASES),)),
            pltpu.SemaphoreType.DMA((len(PHASES),)),
            pltpu.SemaphoreType.REGULAR,
        ],
        compiler_params=pltpu.CompilerParams(
            collective_id=0, has_side_effects=True, vmem_limit_bytes=64 << 20
        ),
        name="fixed_crops",
    )(shuffle_masks, positive, queries, features.reshape(rows, channels), conv_in, conv_mid, conv_out, head, queue)
    return loss.reshape(slots)


def on_device(n_dp, n_bn, *arrays):
    features, conv_in = arrays[0], arrays[2]
    whole_lanes = conv_in.shape[1] % (n_bn * LANES) == 0 and features.shape[2] % (n_bn * LANES) == 0
    if whole_lanes and n_bn % 2 == 0 and n_dp * n_bn % 4 == 0 and n_dp <= features.shape[0] and features.shape[1] == 8:
        return on_device_fixed(n_dp, n_bn, *arrays)
    return on_device_moving(*arrays)


def solution(mesh):
    return jax.shard_map(
        functools.partial(on_device, mesh.shape["dp"], mesh.shape["bn"]),
        mesh=mesh,
        in_specs=(
            P(("dp", "bn"), None, None),
            P(),
            P(),
            P(),
            P(),
            P(),
            P(("dp", "bn"), None),
            P("dp", None),
            P(("dp", "bn")),
        ),
        out_specs=P(("dp", "bn")),
        check_vma=False,
    )
```

```python
import functools

import jax
import jax.numpy as jnp
from jax import lax
from jax.experimental import pallas as pl
from jax.experimental.pallas import tpu as pltpu
from jax.sharding import PartitionSpec as P

EPS_BN = 1e-05
EPS_UNIT = 1e-06
INV_TEMP = 1.0 / 0.07


def partner_2(value, axis, distance):
    return lax.ppermute(value, axis, [(i, i ^ 1 << distance) for i in range(lax.axis_size(axis))])


def unit_rows(values):
    values = values.astype(jnp.float32)
    return values * lax.rsqrt(jnp.sum(values * values, axis=-1, keepdims=True) + EPS_UNIT)


def group_norm(values, row_total):
    first = lax.psum(jnp.sum(values, axis=0), "bn")
    center = first / row_total
    spread = lax.psum(jnp.sum(jnp.square(values - center), axis=0), "bn") / row_total
    return (values - center) * lax.rsqrt(spread + EPS_BN)


def moving_slots(shuffle_masks, level, half):
    flags = jnp.bitwise_and(jnp.right_shift(shuffle_masks, level), 1)
    return jnp.argsort(1 - flags, stable=True)[:half]


def on_device_moving(features, shuffle_masks, conv_in, conv_mid, conv_out, head, queries, queue, positive):
    dp_count = lax.axis_size("dp")
    bn_count = lax.axis_size("bn")
    bit_count = dp_count.bit_length() - 1
    crop_dev, positions, channels = features.shape
    half = crop_dev // 2
    middle = conv_in.shape[1]
    query_unit = unit_rows(queries).astype(jnp.bfloat16)
    query_all = lax.all_gather(query_unit, "dp", axis=0, tiled=True)
    shuffled = features
    for level in range(bit_count):
        moving = moving_slots(shuffle_masks, level, half)
        partner = partner_2(jnp.take(shuffled, moving, axis=0), "dp", level)
        shuffled = shuffled.at[moving].set(partner)
    row_total = crop_dev * positions * bn_count
    flat_rows = shuffled.reshape(crop_dev * positions, channels)
    first_sum = jnp.dot(flat_rows, conv_in, preferred_element_type=jnp.float32)
    first_act = jax.nn.relu(group_norm(first_sum, row_total)).astype(jnp.bfloat16)
    tap_maps = first_act.reshape(crop_dev, positions, middle)
    padded = jnp.pad(tap_maps, ((0, 0), (1, 1), (0, 0)))
    stacked = jnp.concatenate([padded[:, tap : tap + positions, :] for tap in range(3)], axis=2)
    second_sum = jnp.dot(
        stacked.reshape(crop_dev * positions, 3 * middle),
        conv_mid.reshape(3 * middle, middle),
        preferred_element_type=jnp.float32,
    )
    second_act = jax.nn.relu(group_norm(second_sum, row_total)).astype(jnp.bfloat16)
    third_sum = jnp.dot(second_act, conv_out, preferred_element_type=jnp.float32)
    block = jax.nn.relu(group_norm(third_sum, row_total) + flat_rows.astype(jnp.float32)).astype(
        jnp.bfloat16
    )
    pooled = jnp.mean(
        block.reshape(crop_dev, positions, channels).astype(jnp.float32), axis=1
    ).astype(jnp.bfloat16)
    key_unit = unit_rows(jnp.dot(pooled, head, preferred_element_type=jnp.float32)).astype(
        jnp.bfloat16
    )
    for level in range(bit_count):
        moving = moving_slots(shuffle_masks, level, half)
        partner = partner_2(jnp.take(key_unit, moving, axis=0), "dp", level)
        key_unit = key_unit.at[moving].set(partner)
    queue_unit = unit_rows(queue).astype(jnp.bfloat16)
    scores = jnp.dot(query_all, queue_unit.T, preferred_element_type=jnp.float32) * INV_TEMP
    queue_part = jnp.sum(jnp.exp(scores - INV_TEMP), axis=1)
    key_all = lax.all_gather(key_unit, "dp", axis=0, tiled=True)
    slot_of = positive % crop_dev
    column = positive // crop_dev // bn_count
    picked = jnp.take(key_all, column * crop_dev + slot_of, axis=0)
    positive_logit = (
        jnp.sum(query_unit.astype(jnp.float32) * picked.astype(jnp.float32), axis=-1) * INV_TEMP
    )
    negative = lax.psum_scatter(queue_part, "dp", scatter_dimension=0, tiled=True)
    return jnp.log(jnp.exp(positive_logit - INV_TEMP) + negative) + INV_TEMP - positive_logit


MESH = pl.DeviceIdType.MESH
LANES = 128
QUEUE_STEPS = 8
PANELS = 4
PHASES = ("query", "sum1", "norm1", "sum2", "norm2", "sum3", "norm3", "queue", "key")


def fixed_kernel(
    n_dp, n_bn,
    masks_hbm, positive_hbm, queries_hbm, x_hbm, in_hbm, mid_hbm, out_hbm, head_hbm, queue_hbm,
    loss_ref,
    masks, positive, queries,
    x_ref, in_ref, mid_ref, out_ref, head_ref, queue_ref,
    h_ref, wide_ref, mean_ref, scale_ref,
    send1, recv1, own1, stat1, send2, recv2, own2, stat2, send3, recv3, own3, stat3,
    query_own, query_all, part_own, part_all, key_own, key_all,
    load_sem, panel_sem, send_sem, recv_sem,
):
    f32, bf16 = jnp.float32, jnp.bfloat16
    n_dev = n_dp * n_bn
    d = lax.axis_index("dp")
    b = lax.axis_index("bn")
    me = d * n_bn + b
    rows, channels = x_ref.shape
    slots = masks.shape[0]
    cells = rows // slots
    middle = in_ref.shape[1]
    total = float(rows * n_bn)

    panel = channels // PANELS
    panels = [
        pltpu.make_async_copy(
            in_hbm.at[pl.ds(i * panel, panel)], in_ref.at[pl.ds(i * panel, panel)], panel_sem.at[i]
        )
        for i in range(PANELS)
    ]
    loads = [
        pltpu.make_async_copy(src, dst, load_sem.at[i])
        for i, (src, dst) in enumerate(
            [(masks_hbm, masks), (positive_hbm, positive), (queries_hbm, queries), (x_hbm, x_ref), (queue_hbm, queue_ref), (mid_hbm, mid_ref), (out_hbm, out_ref), (head_hbm, head_ref)]
        )
    ]
    for load in loads[:4] + panels:
        load.start()

    barrier = pltpu.get_barrier_semaphore()

    dps = [lax.rem(d + k, n_dp) for k in range(n_dp)]
    bns = [lax.rem(b + k, n_bn) for k in range(n_bn)]
    peers = [(g, j) for g in dps for j in bns][1:]
    for peer in peers:
        pl.semaphore_signal(barrier, inc=1, device_id=peer, device_id_type=MESH)

    n_own = n_dev // 2
    base = n_own // 2
    owner = jnp.logical_and(me >= base, me < base + n_own)
    mine_at = jnp.clip(me - base, 0, n_own - 1)

    for load in loads[:3]:
        load.wait()
    lane = lax.broadcasted_iota(jnp.int32, (slots, slots), 1)
    sub = lax.broadcasted_iota(jnp.int32, (slots, slots), 0)
    mask_row = jnp.zeros((slots, slots), jnp.int32)
    mask_col = jnp.zeros((slots, slots), jnp.int32)
    pos_row = jnp.zeros((1, slots), jnp.int32)
    lane1 = lax.broadcasted_iota(jnp.int32, (1, slots), 1)
    groups = []
    for s in range(slots):
        groups.append(masks[s] ^ d)
        mask_row = jnp.where(lane == s, groups[s], mask_row)
        mask_col = jnp.where(sub == s, groups[s], mask_col)
        pos_row = jnp.where(lane1 == s, positive[s], pos_row)
    same = (mask_row == mask_col).astype(f32)
    local_mean = same / (jnp.sum(same, axis=0, keepdims=True) * float(cells))
    member = (mask_row[:n_dp] == sub[:n_dp]).astype(f32) if n_dp <= slots else None
    counts = []
    for e in range(n_dp):
        want = e ^ lax.div(2 * mine_at, n_bn)
        count = jnp.int32(0)
        for s in range(slots):
            count = count + (masks[s] == want).astype(jnp.int32)
        counts.append((count * cells).astype(f32))

    q = queries[...].astype(f32)
    query_unit = (q * lax.rsqrt(jnp.sum(q * q, axis=-1, keepdims=True) + EPS_UNIT)).astype(bf16)
    query_own[...] = query_unit
    query_all[d] = query_unit

    def push(phase, src, dst, peer):
        i = PHASES.index(phase)
        pltpu.make_async_remote_copy(
            src_ref=src, dst_ref=dst, send_sem=send_sem.at[i], recv_sem=recv_sem.at[i],
            device_id=peer, device_id_type=MESH,
        ).start()

    def to_owners(phase, send, recv):
        for k in range(1, n_own + 1):
            o = lax.rem(me + k, n_own)
            t = o + base
            peer = (lax.div(t, n_bn), lax.rem(t, n_bn))
            if k == n_own - base:
                @pl.when(jnp.logical_not(owner))
                def _():
                    push(phase, send.at[o], recv.at[me], peer)
            else:
                push(phase, send.at[o], recv.at[me], peer)

        @pl.when(owner)
        def _():
            recv[me] = send[mine_at]

    def took(sem, ref, n):
        most = ref.at[pl.ds(0, n)]
        pltpu.make_async_copy(most, most, sem).wait()

    def took_owners(sem, ref):
        @pl.when(owner)
        def _():
            took(sem, ref, n_own - 1)

        @pl.when(jnp.logical_not(owner))
        def _():
            took(sem, ref, n_own)

    def column_peers(phase, src, dst):
        i = PHASES.index(phase)

        for g in dps[1:]:
            pltpu.make_async_remote_copy(
                src_ref=src, dst_ref=dst.at[d],
                send_sem=send_sem.at[i], recv_sem=recv_sem.at[i],
                device_id=(g, b), device_id_type=MESH,
            ).start()

    def arrived(phase, dst):
        most = dst.at[pl.ds(0, dst.shape[0] - 1)]
        pltpu.make_async_copy(most, most, recv_sem.at[PHASES.index(phase)]).wait()

    def sent(phase, dst):
        most = dst.at[pl.ds(0, dst.shape[0] - 1)]
        pltpu.make_async_copy(most, most, send_sem.at[PHASES.index(phase)]).wait()

    def exact(a, c):
        return jnp.dot(a, c, preferred_element_type=f32, precision=lax.Precision.HIGHEST)

    def send_sums(phase, h, send, recv):
        width = h.shape[1]
        block = width // n_bn
        subs = block // LANES
        shaped = h.reshape(slots, cells, width)
        sums = jnp.sum(shaped, axis=1)
        center = exact(local_mean, sums)
        squares = jnp.sum(jnp.square(shaped - center[:, None, :]), axis=1)
        for at, values in ((0, exact(member, sums)), (subs, exact(member, squares))):
            for j in range(n_bn):
                for r in range(subs):
                    low = j * block + r * LANES
                    block_rows = values[:, low : low + LANES]
                    for g in range(n_dp):
                        flat = g * n_bn + j
                        send[flat // 2, flat % 2, at + r, :] = block_rows[g]
        to_owners(phase, send, recv)

    def send_norm(phase_in, phase_out, recv, own, stat):
        @pl.when(owner)
        def _():
            took(recv_sem.at[PHASES.index(phase_in)], recv, n_dev - 1)
            subs = recv.shape[2] // 2
            both = jnp.sum(recv[...], axis=0)
            mean = both[:, :subs] * (1.0 / total)
            spread = both[:, subs:]
            for e in range(n_dp):
                part = recv[e * n_bn : (e + 1) * n_bn][:, :, :subs]
                off = jnp.sum(jnp.square(part - counts[e] * mean[None]), axis=0)
                spread = spread + off / jnp.maximum(counts[e], 1.0)
            own[:, :subs] = mean
            own[:, subs:] = lax.rsqrt(spread * (1.0 / total) + EPS_BN)
            stat[mine_at] = own[...]
            for peer in peers:
                push(phase_out, own, stat.at[mine_at], peer)

    def tables(phase, stat, width):
        took_owners(recv_sem.at[PHASES.index(phase)], stat)
        block = width // n_bn
        subs = block // LANES
        held = stat[...].reshape(n_dp, n_bn, 2 * subs, LANES)
        for j in range(n_bn):
            for r in range(subs):
                low = j * block + r * LANES
                mean_ref[:, low : low + LANES] = held[:, j, r, :]
                scale_ref[:, low : low + LANES] = held[:, j, subs + r, :]

    def slot_row(table, s, width):
        return jnp.broadcast_to(table[pl.ds(groups[s], 1), :width], (cells, width))

    ones = jnp.ones((LANES, LANES), bf16)
    step_rows = queue_ref.shape[0] // QUEUE_STEPS

    def queue_step(c, total_part):
        raw = queue_ref[pl.ds(c * step_rows, step_rows), :].astype(f32)
        square = raw * raw
        high = square.astype(bf16)
        low = (square - high.astype(f32)).astype(bf16)
        norm = jnp.dot(high, ones, preferred_element_type=f32) + jnp.dot(low, ones, preferred_element_type=f32)
        unit = (raw * lax.rsqrt(norm + EPS_UNIT)).astype(bf16)
        flat_queries = query_all[...].reshape(n_dp * slots, query_all.shape[2])
        scores = lax.dot_general(unit, flat_queries, (((1,), (1,)), ((), ())), preferred_element_type=f32)
        terms = jnp.exp(scores * INV_TEMP - INV_TEMP)
        return total_part + jnp.sum(terms.reshape(step_rows // 8, 8, n_dp * slots), axis=0)

    def queue_steps(first, last, total_part):
        return lax.fori_loop(first, last, queue_step, total_part)

    loads[3].wait()
    first = None
    for i in range(PANELS):
        panels[i].wait()
        at = slice(i * panel, (i + 1) * panel)
        term = jnp.dot(x_ref[:, at], in_ref[at], preferred_element_type=f32)
        first = term if first is None else first + term
        if i == 0:
            for load in loads[4:]:
                load.start()
    h_ref[...] = first
    pl.semaphore_wait(barrier, n_dev - 1)
    column_peers("query", query_own, query_all)
    send_sums("sum1", h_ref[...], send1, recv1)
    part = jnp.zeros((8, n_dp * slots), f32)
    loads[4].wait()
    arrived("query", query_all)
    part = queue_steps(0, 1, part)
    send_norm("sum1", "norm1", recv1, own1, stat1)
    loads[5].wait()
    part = queue_steps(1, 3, part)
    tables("norm1", stat1, middle)

    for s in range(slots):
        at = slice(s * cells, (s + 1) * cells)
        h_ref[at] = jax.nn.relu((h_ref[at] - slot_row(mean_ref, s, middle)) * slot_row(scale_ref, s, middle))
    act = h_ref[...]
    cell = lax.broadcasted_iota(jnp.int32, act.shape, 0) % cells
    before = jnp.where(cell == 0, 0.0, pltpu.roll(act, 1, 0)).astype(bf16)
    after = jnp.where(cell == cells - 1, 0.0, pltpu.roll(act, rows - 1, 0)).astype(bf16)
    h_ref[...] = (
        jnp.dot(before, mid_ref[0], preferred_element_type=f32)
        + jnp.dot(act.astype(bf16), mid_ref[1], preferred_element_type=f32)
        + jnp.dot(after, mid_ref[2], preferred_element_type=f32)
    )
    send_sums("sum2", h_ref[...], send2, recv2)
    part = queue_steps(3, 5, part)
    send_norm("sum2", "norm2", recv2, own2, stat2)
    loads[6].wait()
    part = queue_steps(5, 6, part)
    tables("norm2", stat2, middle)

    for s in range(slots):
        at = slice(s * cells, (s + 1) * cells)
        h_ref[at] = jax.nn.relu((h_ref[at] - slot_row(mean_ref, s, middle)) * slot_row(scale_ref, s, middle))
    wide_ref[...] = jnp.dot(h_ref[...].astype(bf16), out_ref[...], preferred_element_type=f32)
    send_sums("sum3", wide_ref[...], send3, recv3)
    part = queue_steps(6, 8, part)
    part_own[...] = jnp.sum(part, axis=0, keepdims=True)
    part_all[d] = part_own[...]
    column_peers("queue", part_own, part_all)
    send_norm("sum3", "norm3", recv3, own3, stat3)
    loads[7].wait()
    tables("norm3", stat3, channels)

    pooled = []
    for i in range(slots // 2):
        at = slice(2 * i * cells, (2 * i + 2) * cells)
        mean = jnp.concatenate([slot_row(mean_ref, 2 * i + o, channels) for o in range(2)], axis=0)
        scale = jnp.concatenate([slot_row(scale_ref, 2 * i + o, channels) for o in range(2)], axis=0)
        block = jax.nn.relu((wide_ref[at] - mean) * scale + x_ref[at].astype(f32)).astype(bf16)
        pooled.append(jnp.mean(block.astype(f32).reshape(2, cells, channels), axis=1))
    pooled = jnp.concatenate(pooled, axis=0).astype(bf16)
    z = jnp.dot(pooled, head_ref[...], preferred_element_type=f32)
    key_own[...] = (z * lax.rsqrt(jnp.sum(z * z, axis=-1, keepdims=True) + EPS_UNIT)).astype(bf16)
    key_all[d] = key_own[...]
    column_peers("key", key_own, key_all)

    arrived("queue", part_all)
    negative_all = jnp.sum(part_all[...], axis=0)
    mine = lax.broadcasted_iota(jnp.int32, (slots, n_dp * slots), 1) == (
        lax.broadcasted_iota(jnp.int32, (slots, n_dp * slots), 0) + d * slots
    )
    negative_col = jnp.sum(jnp.where(mine, negative_all, 0.0), axis=1, keepdims=True)
    negative = jnp.sum(jnp.where(lane == sub, negative_col, 0.0), axis=0, keepdims=True)
    want = (pos_row // (slots * n_bn)) * slots + pos_row % slots

    arrived("key", key_all)
    keys = key_all[...].reshape(n_dp * slots, key_all.shape[2])
    pairs = lax.dot_general(keys, query_own[...], (((1,), (1,)), ((), ())), preferred_element_type=f32)
    chosen = lax.broadcasted_iota(jnp.int32, pairs.shape, 0) == want
    logit = jnp.sum(jnp.where(chosen, pairs, 0.0), axis=0, keepdims=True) * INV_TEMP
    loss_ref[...] = jnp.log(jnp.exp(logit - INV_TEMP) + negative) + INV_TEMP - logit

    for phase, dst in (("query", query_all), ("queue", part_all), ("key", key_all)):
        sent(phase, dst)
    for i, send, recv in ((1, send1, recv1), (3, send2, recv2), (5, send3, recv3)):
        took_owners(send_sem.at[i], send)

        @pl.when(owner)
        def _():
            took(send_sem.at[i + 1], recv, n_dev - 1)


def on_device_fixed(n_dp, n_bn, features, shuffle_masks, conv_in, conv_mid, conv_out, head, queries, queue, positive):
    f32, bf16 = jnp.float32, jnp.bfloat16
    slots, cells, channels = features.shape
    rows = slots * cells
    middle = conv_in.shape[1]
    width = queries.shape[1]
    n_dev = n_dp * n_bn

    def exchange(c):
        tile = (2 * (c // n_bn // LANES), LANES)
        return [
            pltpu.VMEM((n_dev // 2, 2) + tile, f32),
            pltpu.VMEM((n_dev, 2) + tile, f32),
            pltpu.VMEM((2,) + tile, f32),
            pltpu.VMEM((n_dev // 2, 2) + tile, f32),
        ]

    vmem = pl.BlockSpec(memory_space=pltpu.VMEM)
    hbm = pl.BlockSpec(memory_space=pltpu.HBM)
    loss = pl.pallas_call(
        functools.partial(fixed_kernel, n_dp, n_bn),
        out_shape=jax.ShapeDtypeStruct((1, slots), f32),
        in_specs=[hbm] * 9,
        out_specs=vmem,
        scratch_shapes=[
            pltpu.SMEM(shuffle_masks.shape, jnp.int32),
            pltpu.SMEM(positive.shape, jnp.int32),
            pltpu.VMEM(queries.shape, bf16),
            pltpu.VMEM((rows, channels), bf16),
            pltpu.VMEM(conv_in.shape, bf16),
            pltpu.VMEM(conv_mid.shape, bf16),
            pltpu.VMEM(conv_out.shape, bf16),
            pltpu.VMEM(head.shape, bf16),
            pltpu.VMEM(queue.shape, bf16),
            pltpu.VMEM((rows, middle), f32),
            pltpu.VMEM((rows, channels), f32),
            pltpu.VMEM((n_dp, channels), f32),
            pltpu.VMEM((n_dp, channels), f32),
        ]
        + exchange(middle)
        + exchange(middle)
        + exchange(channels)
        + [
            pltpu.VMEM((slots, width), bf16),
            pltpu.VMEM((n_dp, slots, width), bf16),
            pltpu.VMEM((1, n_dp * slots), f32),
            pltpu.VMEM((n_dp, 1, n_dp * slots), f32),
            pltpu.VMEM((slots, width), bf16),
            pltpu.VMEM((n_dp, slots, width), bf16),
            pltpu.SemaphoreType.DMA((8,)),
            pltpu.SemaphoreType.DMA((PANELS,)),
            pltpu.SemaphoreType.DMA((len(PHASES),)),
            pltpu.SemaphoreType.DMA((len(PHASES),)),
        ],
        compiler_params=pltpu.CompilerParams(
            collective_id=0, has_side_effects=True, vmem_limit_bytes=64 << 20
        ),
        name="fixed_crops",
    )(shuffle_masks, positive, queries, features.reshape(rows, channels), conv_in, conv_mid, conv_out, head, queue)
    return loss.reshape(slots)


def on_device(n_dp, n_bn, *arrays):
    features, conv_in = arrays[0], arrays[2]
    whole_lanes = conv_in.shape[1] % (n_bn * LANES) == 0 and features.shape[2] % (n_bn * LANES) == 0
    if whole_lanes and n_bn % 2 == 0 and n_dp * n_bn % 4 == 0 and n_dp <= features.shape[0] and features.shape[1] == 8:
        return on_device_fixed(n_dp, n_bn, *arrays)
    return on_device_moving(*arrays)


def solution(mesh):
    return jax.shard_map(
        functools.partial(on_device, mesh.shape["dp"], mesh.shape["bn"]),
        mesh=mesh,
        in_specs=(
            P(("dp", "bn"), None, None),
            P(),
            P(),
            P(),
            P(),
            P(),
            P(("dp", "bn"), None),
            P("dp", None),
            P(("dp", "bn")),
        ),
        out_specs=P(("dp", "bn")),
        check_vma=False,
    )
```
